32 devices in a mesh: groups: 2 (over y), tile: 4 (over z), image: 4 (over x, core).
Axes of the slice: x: 2, y: 2, z: 4, core: 2. Of those that a mesh axis runs over, the one named last changes fastest.
Arguments:
- images: bfloat16 [8, 16, 64, 256], P(('groups', 'image'), 'tile'), parts along dimension 0, may hold values from -12 to 12
- cotangent: bfloat16 [8, 16, 64, 256], P(('groups', 'image'), 'tile'), parts along dimension 0, may hold values from -12 to 12
- timesteps: int32 [8], P(('groups', 'image')), parts along dimension 0, may hold values from 0 to 999
- class_ids: int32 [8], P(('groups', 'image')), parts along dimension 0, may hold values from 0 to 999
- norm_gain: float32 [256], replicated, may hold values from 0.25 to 1.75
- norm_bias: float32 [256], replicated, may hold values from -3 to 3
- conv_first: bfloat16 [3, 3, 256, 256], replicated, may hold values from -0.125 to 0.125
- conv_second: bfloat16 [3, 3, 256, 256], replicated, may hold values from -0.125 to 0.125
- time_weight: bfloat16 [256, 1024], P(None, 'tile'), may hold values from -0.375 to 0.375
- time_bias: float32 [1024], P('tile'), may hold values from -3 to 3
- class_table: bfloat16 [1000, 1024], P(None, 'tile'), may hold values from -5 to 5
- adaptive_weight: bfloat16 [1024, 512], P('tile'), may hold values from -0.1875 to 0.1875
- adaptive_bias: float32 [512], replicated, may hold values from -2 to 2
Outputs:
- branch: bfloat16 [8, 16, 64, 256], P(('groups', 'image'), 'tile'), parts along dimension 0
- input_grad: bfloat16 [8, 16, 64, 256], P(('groups', 'image'), 'tile'), parts along dimension 0
- grad_adaptive_weight: float32 [2048, 512], P(('groups', 'tile')), parts along dimension 0
- grad_adaptive_bias: float32 [1024], P('groups'), parts along dimension 0
The draws below stay inside these ranges and needn't reach their ends.
There are 2 independent parts, one for each index of `groups`. The reference program is written for one: setup_inputs(seed, part) draws one part's arguments, and reference() takes and returns one part's arrays. A program takes and returns all parts, laid end to end along the dimension named above; an argument that names none is the same for every part. Nothing has to cross between parts.
All inputs are finite; a program needn't handle non-finite values.
Results may differ from the reference program's by a relative error of at most 0.013.
Values may be sent and summed in bfloat16 or wider, within the bound.
A program may use at most 64 MiB of HBM per device.

```python
import math
import jax
import jax.numpy as jnp
from jax import lax

C = 256
EMB = 1024
FREQ = 256
CLASSES = 1000
GN_GROUPS = 32
COLS = 64
IMAGES = 4
H = 16


def scaled_field(key, offset_tag):
    folded = jax.random.fold_in(key, offset_tag)
    sample_key, row_key, chan_key = jax.random.split(folded, 3)
    extent = (IMAGES, H, COLS, C)
    sample = jnp.clip(jax.random.normal(sample_key, extent, jnp.float32), -4.0, 4.0)
    rising = 3.0 ** (jnp.arange(H, dtype=jnp.float32) / (H - 1))
    row_scale = rising[None, :] * jnp.exp(jax.random.uniform(row_key, (IMAGES, H), jnp.float32, 0.0, math.log(3.3))) / math.sqrt(10.0)
    chan_scale = jnp.exp(jax.random.uniform(chan_key, (IMAGES, C), jnp.float32, math.log(0.316), math.log(3.16)))
    return jnp.clip(sample * row_scale[:, :, None, None] * chan_scale[:, None, None, :], -12.0, 12.0)


def draw_images(key, part):
    return scaled_field(key, 11).astype(jnp.bfloat16)


def draw_cotangent(key, part):
    return scaled_field(key, 23).astype(jnp.bfloat16)


def with_ends(result, stream_key, smallest, top_value):
    spot = [jax.random.randint(jax.random.fold_in(stream_key, axis), (), 0, length) for axis, length in enumerate(result.shape)]
    main_axis = result.shape.index(max(result.shape))
    next_to = spot[:main_axis] + [(spot[main_axis] + 1) % result.shape[main_axis]] + spot[main_axis + 1:]
    return result.at[tuple(spot)].set(smallest).at[tuple(next_to)].set(top_value)


def steps_of(key, dims, cuts, least, top_value):
    def one(position, shards_of):
        heights = jax.random.uniform(jax.random.fold_in(jax.random.fold_in(key, 6), position), (shards_of,), jnp.float32, least / len(cuts), top_value / len(cuts))
        return jnp.repeat(jnp.exp(heights), dims[position] // shards_of).reshape((-1,) + (1,) * (len(dims) - position - 1))

    level = one(*cuts[0])
    for cut in cuts[1:]:
        level = level * one(*cut)
    return level


def gaussian(key, shape, width, bound, pieces=(), kind=jnp.bfloat16):
    entries = width * jax.random.normal(key, shape, jnp.float32)
    if pieces:
        entries = entries * steps_of(key, shape, pieces, -0.22, 0.18)
    return jnp.clip(entries, -bound, bound).astype(kind)


def setup_inputs(seed: int = 0, part: int = 0) -> dict:
    seeds = jax.random.split(jax.random.key(seed), 14)
    part_keys = jax.random.split(jax.random.fold_in(seeds[13], part), 14)
    images = draw_images(jax.random.fold_in(jax.random.fold_in(seeds[13], part), 71), part)
    cotangent = draw_cotangent(jax.random.fold_in(jax.random.fold_in(seeds[13], part), 71), part)
    timesteps = with_ends(jax.random.randint(part_keys[2], (IMAGES,), 0, 1000), jax.random.fold_in(part_keys[2], 1), 0, 999).astype(jnp.int32)
    class_ids = with_ends(jax.random.randint(part_keys[3], (IMAGES,), 0, CLASSES), jax.random.fold_in(part_keys[3], 1), 0, CLASSES - 1).astype(jnp.int32)
    norm_gain = jnp.clip(1.0 + 0.15 * jax.random.normal(seeds[4], (C,), jnp.float32), 0.25, 1.75)
    norm_bias = gaussian(seeds[5], (C,), 0.5, 3.0, (), jnp.float32)
    conv_first = gaussian(seeds[6], (3, 3, C, C), (9 * C) ** -0.5, 0.125)
    conv_second = gaussian(seeds[7], (3, 3, C, C), (9 * C) ** -0.5, 0.125)
    time_weight = gaussian(seeds[8], (FREQ, EMB), FREQ ** -0.5, 0.375, ((1, 4),))
    time_bias = gaussian(seeds[9], (EMB,), 0.5, 3.0, ((0, 4),), jnp.float32)
    class_table = gaussian(seeds[10], (CLASSES, EMB), 1.0, 5.0, ((1, 4),))
    adaptive_weight = gaussian(seeds[11], (EMB, 2 * C), EMB ** -0.5, 0.1875, ((0, 4),))
    adaptive_bias = gaussian(seeds[12], (2 * C,), 0.3, 2.0, (), jnp.float32)
    return {"images": images, "cotangent": cotangent, "timesteps": timesteps, "class_ids": class_ids, "norm_gain": norm_gain, "norm_bias": norm_bias, "conv_first": conv_first, "conv_second": conv_second, "time_weight": time_weight, "time_bias": time_bias, "class_table": class_table, "adaptive_weight": adaptive_weight, "adaptive_bias": adaptive_bias}


EPSILON = 1e-05

def rounded(values):
    return lax.optimization_barrier(values.astype(jnp.bfloat16)).astype(jnp.float32)

def conv_same(values, kernel):
    return lax.conv_general_dilated(values[None], kernel.astype(jnp.float32), (1, 1), 'SAME', dimension_numbers=('NHWC', 'HWIO', 'NHWC'), precision=lax.Precision.HIGHEST)[0]

def group_mean(values):
    per_group = values.reshape(-1, GN_GROUPS, C // GN_GROUPS).mean(axis=(0, 2))
    return jnp.repeat(per_group, C // GN_GROUPS)

def normalize(values):
    centred = values - group_mean(values)
    inverse = lax.rsqrt(group_mean(centred * centred) + EPSILON)
    return (centred * inverse, inverse)

def norm_backward(grad_norm, normed, inverse):
    return inverse * (grad_norm - group_mean(grad_norm) - normed * group_mean(grad_norm * normed))

def silu_grad(pre_values):
    sigma = jax.nn.sigmoid(pre_values)
    return sigma * (1.0 + pre_values * (1.0 - sigma))

def reference(images, cotangent, timesteps, class_ids, norm_gain, norm_bias, conv_first, conv_second, time_weight, time_bias, class_table, adaptive_weight, adaptive_bias):
    half_freq = FREQ // 2
    frequencies = jnp.exp(-math.log(10000.0) * jnp.arange(half_freq, dtype=jnp.float32) / half_freq)
    angles = timesteps.astype(jnp.float32)[:, None] * frequencies[None]
    sinusoid = jnp.concatenate([jnp.cos(angles), jnp.sin(angles)], axis=1)
    hidden = jnp.dot(sinusoid, time_weight.astype(jnp.float32), precision=lax.Precision.HIGHEST) + time_bias.astype(jnp.float32)
    onehot = (class_ids[:, None] == jnp.arange(CLASSES, dtype=jnp.int32)[None]).astype(jnp.float32)
    embedding = jax.nn.silu(hidden) + jnp.dot(onehot, class_table.astype(jnp.float32), precision=lax.Precision.HIGHEST)
    activated = jax.nn.silu(embedding)
    modulation = jnp.dot(activated, adaptive_weight.astype(jnp.float32), precision=lax.Precision.HIGHEST) + adaptive_bias.astype(jnp.float32)
    flipped_first = jnp.flip(conv_first, (0, 1)).transpose(0, 1, 3, 2)
    flipped_second = jnp.flip(conv_second, (0, 1)).transpose(0, 1, 3, 2)
    gain = norm_gain.astype(jnp.float32)
    bias_term = norm_bias.astype(jnp.float32)

    def one_image(inputs):
        picture, grad_out, modul_row = inputs
        normed_first, inverse_first = normalize(picture.astype(jnp.float32))
        pre_first = normed_first * gain + bias_term
        active_first = rounded(jax.nn.silu(pre_first))
        hidden_first = rounded(conv_same(active_first, conv_first))
        normed_second, inverse_second = normalize(hidden_first)
        factor = 1.0 + modul_row[:C]
        pre_second = normed_second * factor + modul_row[C:]
        active_second = rounded(jax.nn.silu(pre_second))
        branch = conv_same(active_second, conv_second).astype(jnp.bfloat16)
        grad_active = conv_same(grad_out.astype(jnp.float32), flipped_second)
        grad_pre = grad_active * silu_grad(pre_second)
        grad_scale = lax.optimization_barrier(jnp.sum(grad_pre * normed_second, axis=(0, 1)))
        grad_shift = lax.optimization_barrier(jnp.sum(grad_pre, axis=(0, 1)))
        grad_hidden = rounded(norm_backward(grad_pre * factor, normed_second, inverse_second))
        grad_active_first = conv_same(grad_hidden, flipped_first)
        grad_first = grad_active_first * silu_grad(pre_first) * gain
        input_grad = norm_backward(grad_first, normed_first, inverse_first).astype(jnp.bfloat16)
        return (branch, input_grad, jnp.concatenate([grad_scale, grad_shift]))
    branch, input_grad, pairs = lax.map(one_image, (images, cotangent, modulation))
    grad_weight = jnp.dot(activated.T, pairs, precision=lax.Precision.HIGHEST)
    grad_bias = lax.optimization_barrier(jnp.sum(pairs, axis=0))
    return (branch, input_grad, grad_weight, grad_bias)
```

```python
import functools
import math

import jax
import jax.numpy as jnp
from jax import lax
from jax.experimental import pallas as pl
from jax.experimental.pallas import tpu as pltpu
from jax.sharding import PartitionSpec as P

GN_GROUPS = 32
EPSILON = 1e-05
MESH = pl.DeviceIdType.MESH
F32 = jnp.float32
BF16 = jnp.bfloat16
REACH = 2
HIGHEST = lax.Precision.HIGHEST


def group_spread(values, width):
    count = values.shape[-1]
    lane = lax.broadcasted_iota(jnp.int32, values.shape, values.ndim - 1)
    step = 1
    while step < width:
        up = pltpu.roll(values, step, values.ndim - 1)
        down = pltpu.roll(values, count - step, values.ndim - 1)
        values = values + jnp.where((lane & step) != 0, up, down)
        step *= 2
    return values


def silu_slope(pre, sigma):
    return sigma * (1.0 + pre * (1.0 - sigma))


def column_sums(first, second):
    return jnp.concatenate(
        [jnp.sum(first, axis=0, keepdims=True), jnp.sum(second, axis=0, keepdims=True)], axis=0
    )


def kernel(
    n, m,
    steps_ref, ids_ref, gain_ref, bias_ref, tbias_ref, abias_ref,
    images_hbm, cot_hbm, first_hbm, second_hbm, tweight_hbm, table_hbm, aweight_hbm,
    branch_hbm, igrad_hbm, wgrad_hbm, bgrad_ref,
    images, cot, first, second, tweight, table, aweight,
    wide_first, wide_cot, wide_second, wide_hidden,
    hidden, gact, nsecond, gpre, nfirst, slope, branch, igrad, wgrad,
    slots, acts, pairs,
    load_sem, store_sem, halo_send, halo_recv, send_sem, recv_sem,
    act_send, act_recv, pair_send, pair_recv,
):
    me = lax.axis_index("tile")
    mine = lax.axis_index("image")
    rows, cols, channels = images_hbm.shape[1:]
    width = channels // GN_GROUPS
    cells = float(rows * cols * n * width)
    own = rows * cols
    rim = cols
    above, below = me > 0, me < n - 1

    loads = [
        pltpu.make_async_copy(source, target, load_sem.at[k])
        for k, (source, target) in enumerate(
            [
                (images_hbm.at[0], images.at[pl.ds(REACH, rows)]),
                (cot_hbm.at[0], cot.at[pl.ds(REACH, rows)]),
                (tweight_hbm, tweight),
                (table_hbm, table),
                (aweight_hbm, aweight),
                (first_hbm, first),
                (second_hbm, second),
            ]
        )
    ]
    for load in loads:
        load.start()

    barrier = pltpu.get_barrier_semaphore()
    for k in range(1, n):
        pl.semaphore_signal(
            barrier, inc=1, device_id={"tile": lax.rem(me + k, n)}, device_id_type=MESH
        )
    for k in range(1, m):
        pl.semaphore_signal(
            barrier, inc=1, device_id={"image": lax.rem(mine + k, m)}, device_id_type=MESH
        )

    def tile_copy(stage, k, arriving):
        peer = lax.rem(me + k, n)
        slot = lax.rem(me + n - k, n) if arriving else me
        return pltpu.make_async_remote_copy(
            src_ref=slots.at[stage, slot],
            dst_ref=slots.at[stage, slot],
            send_sem=send_sem.at[stage, k],
            recv_sem=recv_sem.at[stage, k],
            device_id={"tile": peer},
            device_id_type=MESH,
        )

    def share(stage, value):
        slots[stage, me] = value
        for k in range(1, n):
            tile_copy(stage, k, False).start()

    def total(stage):
        for k in range(1, n):
            tile_copy(stage, k, True).wait_recv()
        summed = slots[stage, 0]
        for k in range(1, n):
            summed = summed + slots[stage, k]
        return summed

    def image_copy(buffer, sends, receives, k, arriving):
        peer = lax.rem(mine + k, m)
        slot = lax.rem(mine + m - k, m) if arriving else mine
        return pltpu.make_async_remote_copy(
            src_ref=buffer.at[slot],
            dst_ref=buffer.at[slot],
            send_sem=sends.at[k],
            recv_sem=receives.at[k],
            device_id={"image": peer},
            device_id_type=MESH,
        )

    def halo_copy(which, buffer, up):
        source = pl.ds(REACH, REACH) if up else pl.ds(rows, REACH)
        target = pl.ds(rows + REACH, REACH) if up else pl.ds(0, REACH)
        return pltpu.make_async_remote_copy(
            src_ref=buffer.at[source],
            dst_ref=buffer.at[target],
            send_sem=halo_send.at[which, int(up)],
            recv_sem=halo_recv.at[which, int(up)],
            device_id={"tile": me - 1 if up else me + 1},
            device_id_type=MESH,
        )

    def flat(buffer, start, count):
        return buffer[pl.ds(start, count)].reshape(count * cols, channels).astype(F32)

    def widen(wide, start, values):
        count = values.shape[0]
        column = lax.rem(lax.broadcasted_iota(jnp.int32, values.shape, 0), cols)
        before = jnp.where(column == 0, 0.0, pltpu.roll(values, 1, 0))
        after = jnp.where(column == cols - 1, 0.0, pltpu.roll(values, count - 1, 0))
        at = pl.ds(start * cols, count)
        wide[at, 0:channels] = before.astype(BF16)
        wide[at, channels : 2 * channels] = values.astype(BF16)
        wide[at, 2 * channels : 3 * channels] = after.astype(BF16)

    def conv(wide, start, count, weight):
        summed = None
        for i in range(3):
            product = jnp.dot(
                wide[pl.ds((start + i) * cols, count * cols), :],
                weight[i].reshape(3 * channels, channels),
                preferred_element_type=F32,
            )
            summed = product if summed is None else summed + product
        return summed

    def conv_back(wide, start, count, weight):
        summed = None
        for i in range(3):
            for j in range(3):
                product = lax.dot_general(
                    wide[pl.ds((start + i) * cols, count * cols), j * channels : (j + 1) * channels],
                    weight[2 - i, 2 - j],
                    (((1,), (1,)), ((), ())),
                    preferred_element_type=F32,
                )
                summed = product if summed is None else summed + product
        return summed

    def moments(summed):
        spread = group_spread(summed, width) / cells
        centre = spread[0:1]
        variance = jnp.maximum(spread[1:2] - centre * centre, 0.0)
        return centre, lax.rsqrt(variance + EPSILON)

    loads[0].wait()
    values = flat(images, REACH, rows)
    sums = column_sums(values, values * values)
    loads[1].wait()
    pl.semaphore_wait(barrier, n - 1 + m - 1)
    share(0, sums)
    for which, buffer in enumerate((images, cot)):

        @pl.when(above)
        def _():
            halo_copy(which, buffer, True).start()

        @pl.when(below)
        def _():
            halo_copy(which, buffer, False).start()

        @pl.when(jnp.logical_not(above))
        def _():
            buffer[pl.ds(0, REACH)] = jnp.zeros((REACH, cols, channels), BF16)

        @pl.when(jnp.logical_not(below))
        def _():
            buffer[pl.ds(rows + REACH, REACH)] = jnp.zeros((REACH, cols, channels), BF16)

    for k in (2, 3, 4):
        loads[k].wait()
    half = tweight.shape[0] // 2
    index = lax.broadcasted_iota(jnp.int32, (half, 1), 0).astype(F32)
    angles = steps_ref[0].astype(F32) * jnp.exp(-math.log(10000.0) * index / half)
    pre_time = (
        jnp.sum(jnp.cos(angles) * tweight[0:half].astype(F32), axis=0, keepdims=True)
        + jnp.sum(jnp.sin(angles) * tweight[half:].astype(F32), axis=0, keepdims=True)
        + tbias_ref[...]
    )
    entry = lax.broadcasted_iota(jnp.int32, table.shape, 0) == ids_ref[0]
    picked = jnp.sum(jnp.where(entry, table[...].astype(F32), 0.0), axis=0, keepdims=True)
    embedding = pre_time * jax.nn.sigmoid(pre_time) + picked
    activated = embedding * jax.nn.sigmoid(embedding)
    acts[mine] = activated
    for k in range(1, m):
        image_copy(acts, act_send, act_recv, k, False).start()
    partial = jnp.dot(
        jnp.broadcast_to(activated, (8, activated.shape[1])),
        aweight[...].astype(F32),
        precision=HIGHEST,
        preferred_element_type=F32,
    )[0:1]
    share(1, jnp.concatenate([partial[:, :channels], partial[:, channels:]], axis=0))

    gain, bias = gain_ref[...], bias_ref[...]
    centre, inverse_first = moments(total(0))

    def first_activation(normed):
        pre = normed * gain + bias
        return pre, jax.nn.sigmoid(pre)

    values = (flat(images, REACH, rows) - centre) * inverse_first
    pre, sigma = first_activation(values)
    widen(wide_first, REACH, pre * sigma)

    def halo_wait(which, buffer):
        @pl.when(below)
        def _():
            halo_copy(which, buffer, True).wait_recv()

        @pl.when(above)
        def _():
            halo_copy(which, buffer, False).wait_recv()

    halo_wait(0, images)
    for start, inside in ((0, above), (rows + REACH, below)):
        rim_values = (flat(images, start, REACH) - centre) * inverse_first
        rim_pre, rim_sigma = first_activation(rim_values)
        widen(wide_first, start, jnp.where(inside, rim_pre * rim_sigma, 0.0))
    loads[5].wait()
    centre_rows = conv(wide_first, 1, rows, first).astype(BF16).astype(F32)
    share(2, column_sums(centre_rows, centre_rows * centre_rows))
    hidden[pl.ds(rim, own)] = centre_rows

    for row in (0, rows + 1):
        hidden[pl.ds(row * cols, cols)] = conv(wide_first, row, 1, first).astype(BF16).astype(F32)
    halo_wait(1, cot)
    widen(wide_cot, 0, flat(cot, 0, rows + 2 * REACH))
    loads[6].wait()
    gact[...] = conv_back(wide_cot, 0, rows + 2, second)
    values = (flat(images, REACH, rows) - centre) * inverse_first
    pre, sigma = first_activation(values)
    nfirst[...] = values
    slope[...] = silu_slope(pre, sigma) * gain

    modulation = total(1)
    factor = 1.0 + (modulation[0:1] + abias_ref[:, :channels])
    shift = modulation[1:2] + abias_ref[:, channels:]
    centre, inverse_second = moments(total(2))
    for start, count, inside in ((1, rows, None), (0, 1, above), (rows + 1, 1, below)):
        at = pl.ds(start * cols, count * cols)
        normed = (hidden[at] - centre) * inverse_second
        pre = normed * factor + shift
        sigma = jax.nn.sigmoid(pre)
        back = gact[at] * silu_slope(pre, sigma)
        if inside is None:
            share(3, column_sums(back * normed, back))
        active = pre * sigma
        if inside is not None:
            active = jnp.where(inside, active, 0.0)
        widen(wide_second, start, active)
        nsecond[at] = normed
        gpre[at] = back

    branch[...] = conv(wide_second, 0, rows, second).astype(BF16).reshape(rows, cols, channels)
    stores = [pltpu.make_async_copy(branch, branch_hbm.at[0], store_sem.at[0])]
    stores[0].start()

    sums = total(3)
    spread = group_spread(sums * factor, width) / cells
    paired_mean, plain_mean = spread[0:1], spread[1:2]
    for start, count, inside in ((1, rows, None), (0, 1, above), (rows + 1, 1, below)):
        at = pl.ds(start * cols, count * cols)
        back = inverse_second * (gpre[at] * factor - plain_mean - nsecond[at] * paired_mean)
        if inside is not None:
            back = jnp.where(inside, back, 0.0)
        widen(wide_hidden, start, back)
    pairs[mine] = sums
    for k in range(1, m):
        image_copy(pairs, pair_send, pair_recv, k, False).start()
    back = conv_back(wide_hidden, 0, rows, first) * slope[...]
    normed = nfirst[...]
    share(4, column_sums(back, back * normed))

    for k in range(1, m):
        image_copy(acts, act_send, act_recv, k, True).wait_recv()
        image_copy(pairs, pair_send, pair_recv, k, True).wait_recv()
    extra = (-m) % 8

    def stacked(pieces):
        if extra:
            pieces = pieces + [jnp.zeros((extra, pieces[0].shape[1]), F32)]
        return jnp.concatenate(pieces, axis=0)

    left = stacked([acts[k] for k in range(m)])
    for part in range(2):
        right = stacked([pairs[k][part : part + 1] for k in range(m)])
        columns = slice(part * channels, (part + 1) * channels)
        wgrad[:, columns] = lax.dot_general(
            left, right, (((0,), (0,)), ((), ())), precision=HIGHEST, preferred_element_type=F32
        )
        bgrad_ref[:, columns] = jnp.sum(right, axis=0, keepdims=True)
    stores.append(pltpu.make_async_copy(wgrad, wgrad_hbm, store_sem.at[1]))
    stores[1].start()

    spread = group_spread(total(4), width) / cells
    result = inverse_first * (back - spread[0:1] - normed * spread[1:2])
    igrad[...] = result.astype(BF16).reshape(rows, cols, channels)
    stores.append(pltpu.make_async_copy(igrad, igrad_hbm.at[0], store_sem.at[2]))
    stores[2].start()

    for stage in range(5):
        for k in range(1, n):
            tile_copy(stage, k, False).wait_send()
    for k in range(1, m):
        image_copy(acts, act_send, act_recv, k, False).wait_send()
        image_copy(pairs, pair_send, pair_recv, k, False).wait_send()
    for which, buffer in enumerate((images, cot)):

        @pl.when(above)
        def _():
            halo_copy(which, buffer, True).wait_send()

        @pl.when(below)
        def _():
            halo_copy(which, buffer, False).wait_send()

    for store in stores:
        store.wait()


def body(
    n, m,
    images, cotangent, timesteps, class_ids, norm_gain, norm_bias, conv_first, conv_second,
    time_weight, time_bias, class_table, adaptive_weight, adaptive_bias,
):
    count, rows, cols, channels = images.shape
    assert count == 1 and rows >= REACH
    emb = time_weight.shape[1]
    smem = pl.BlockSpec(memory_space=pltpu.SMEM)
    vmem = pl.BlockSpec(memory_space=pltpu.VMEM)
    anywhere = pl.BlockSpec(memory_space=pl.ANY)
    padded = rows + 2 * REACH
    own, more, most = rows * cols, (rows + 2) * cols, padded * cols
    dma = pltpu.SemaphoreType.DMA
    branch, igrad, wgrad, bgrad = pl.pallas_call(
        functools.partial(kernel, n, m),
        out_shape=(
            jax.ShapeDtypeStruct(images.shape, BF16),
            jax.ShapeDtypeStruct(images.shape, BF16),
            jax.ShapeDtypeStruct((emb, 2 * channels), F32),
            jax.ShapeDtypeStruct((1, 2 * channels), F32),
        ),
        in_specs=[smem] * 2 + [vmem] * 4 + [anywhere] * 7,
        out_specs=(anywhere, anywhere, anywhere, vmem),
        scratch_shapes=[
            pltpu.VMEM((padded, cols, channels), BF16),
            pltpu.VMEM((padded, cols, channels), BF16),
            pltpu.VMEM(conv_first.shape, BF16),
            pltpu.VMEM(conv_second.shape, BF16),
            pltpu.VMEM(time_weight.shape, BF16),
            pltpu.VMEM(class_table.shape, BF16),
            pltpu.VMEM(adaptive_weight.shape, BF16),
            pltpu.VMEM((most, 3 * channels), BF16),
            pltpu.VMEM((most, 3 * channels), BF16),
            pltpu.VMEM((more, 3 * channels), BF16),
            pltpu.VMEM((more, 3 * channels), BF16),
            pltpu.VMEM((more, channels), F32),
            pltpu.VMEM((more, channels), F32),
            pltpu.VMEM((more, channels), F32),
            pltpu.VMEM((more, channels), F32),
            pltpu.VMEM((own, channels), F32),
            pltpu.VMEM((own, channels), F32),
            pltpu.VMEM((rows, cols, channels), BF16),
            pltpu.VMEM((rows, cols, channels), BF16),
            pltpu.VMEM((emb, 2 * channels), F32),
            pltpu.VMEM((5, n, 2, channels), F32),
            pltpu.VMEM((m, 1, emb), F32),
            pltpu.VMEM((m, 2, channels), F32),
            dma((7,)),
            dma((3,)),
            dma((2, 2)),
            dma((2, 2)),
            dma((5, n)),
            dma((5, n)),
            dma((m,)),
            dma((m,)),
            dma((m,)),
            dma((m,)),
        ],
        compiler_params=pltpu.CompilerParams(collective_id=0, has_side_effects=True),
    )(
        timesteps, class_ids, norm_gain[None], norm_bias[None], time_bias[None],
        adaptive_bias[None], images, cotangent, conv_first, conv_second, time_weight,
        class_table, adaptive_weight,
    )
    return branch, igrad, wgrad, bgrad[0]


def solution(mesh):
    return jax.shard_map(
        functools.partial(body, mesh.shape["tile"], mesh.shape["image"]),
        mesh=mesh,
        in_specs=(
            P(("groups", "image"), "tile", None, None),
            P(("groups", "image"), "tile", None, None),
            P(("groups", "image")),
            P(("groups", "image")),
            P(),
            P(),
            P(),
            P(),
            P(None, "tile"),
            P("tile"),
            P(None, "tile"),
            P("tile", None),
            P(),
        ),
        out_specs=(
            P(("groups", "image"), "tile", None, None),
            P(("groups", "image"), "tile", None, None),
            P(("groups", "tile"), None),
            P("groups"),
        ),
        check_vma=False,
    )
```

```python
import functools
import math

import jax
import jax.numpy as jnp
from jax import lax
from jax.experimental import pallas as pl
from jax.experimental.pallas import tpu as pltpu
from jax.sharding import PartitionSpec as P

GN_GROUPS = 32
EPSILON = 1e-05
MESH = pl.DeviceIdType.MESH
F32 = jnp.float32
BF16 = jnp.bfloat16
GRANT = 24 << 20
REACH = 2
HIGHEST = lax.Precision.HIGHEST


def group_spread(values, width):
    count = values.shape[-1]
    lane = lax.broadcasted_iota(jnp.int32, values.shape, values.ndim - 1)
    step = 1
    while step < width:
        up = pltpu.roll(values, step, values.ndim - 1)
        down = pltpu.roll(values, count - step, values.ndim - 1)
        values = values + jnp.where((lane & step) != 0, up, down)
        step *= 2
    return values


def silu_slope(pre, sigma):
    return sigma * (1.0 + pre * (1.0 - sigma))


def column_sums(first, second):
    return jnp.concatenate(
        [jnp.sum(first, axis=0, keepdims=True), jnp.sum(second, axis=0, keepdims=True)], axis=0
    )


def kernel(
    n, m,
    steps_ref, ids_ref, gain_hbm, bias_hbm, tbias_hbm, abias_hbm,
    images_hbm, cot_hbm, first_hbm, second_hbm, tweight_hbm, table_hbm, aweight_hbm,
    branch, igrad, acts_out, pairs_out,
    images, cot, first, second, tweight, table, aweight,
    gain_ref, bias_ref, tbias_ref, abias_ref,
    wide_first, wide_cot, wide_second, wide_hidden,
    hidden, gact, nsecond, gpre, nfirst, slope,
    slots, acts, pairs,
    load_sem, halo_send, halo_recv, send_sem, recv_sem,
    act_send, act_recv, pair_send, pair_recv,
):
    me = lax.axis_index("tile")
    mine = lax.axis_index("image")
    rows, cols, channels = images_hbm.shape[1:]
    width = channels // GN_GROUPS
    cells = float(rows * cols * n * width)
    own = rows * cols
    rim = cols
    above, below = me > 0, me < n - 1

    loads = [
        pltpu.make_async_copy(source, target, load_sem.at[k])
        for k, (source, target) in enumerate(
            [
                (images_hbm.at[0], images.at[pl.ds(REACH, rows)]),
                (cot_hbm.at[0], cot.at[pl.ds(REACH, rows)]),
                (tweight_hbm, tweight),
                (table_hbm, table),
                (aweight_hbm, aweight),
                (first_hbm, first),
                (second_hbm, second),
                (gain_hbm, gain_ref),
                (bias_hbm, bias_ref),
                (tbias_hbm, tbias_ref),
                (abias_hbm, abias_ref),
            ]
        )
    ]
    for load in loads:
        load.start()

    barrier = pltpu.get_barrier_semaphore()
    for k in range(1, n):
        pl.semaphore_signal(
            barrier, inc=1, device_id={"tile": lax.rem(me + k, n)}, device_id_type=MESH
        )
    for k in range(1, m):
        pl.semaphore_signal(
            barrier, inc=1, device_id={"image": lax.rem(mine + k, m)}, device_id_type=MESH
        )

    def tile_copy(stage, k, arriving):
        peer = lax.rem(me + k, n)
        slot = lax.rem(me + n - k, n) if arriving else me
        return pltpu.make_async_remote_copy(
            src_ref=slots.at[stage, slot],
            dst_ref=slots.at[stage, slot],
            send_sem=send_sem.at[stage, k],
            recv_sem=recv_sem.at[stage, k],
            device_id={"tile": peer},
            device_id_type=MESH,
        )

    def share(stage, value):
        slots[stage, me] = value
        for k in range(1, n):
            tile_copy(stage, k, False).start()

    def total(stage):
        for k in range(1, n):
            tile_copy(stage, k, True).wait_recv()
        summed = slots[stage, 0]
        for k in range(1, n):
            summed = summed + slots[stage, k]
        return summed

    def image_copy(buffer, sends, receives, k, arriving):
        peer = lax.rem(mine + k, m)
        slot = lax.rem(mine + m - k, m) if arriving else mine
        return pltpu.make_async_remote_copy(
            src_ref=buffer.at[slot],
            dst_ref=buffer.at[slot],
            send_sem=sends.at[k],
            recv_sem=receives.at[k],
            device_id={"image": peer},
            device_id_type=MESH,
        )

    def halo_copy(which, buffer, up):
        source = pl.ds(REACH, REACH) if up else pl.ds(rows, REACH)
        target = pl.ds(rows + REACH, REACH) if up else pl.ds(0, REACH)
        return pltpu.make_async_remote_copy(
            src_ref=buffer.at[source],
            dst_ref=buffer.at[target],
            send_sem=halo_send.at[which, int(up)],
            recv_sem=halo_recv.at[which, int(up)],
            device_id={"tile": me - 1 if up else me + 1},
            device_id_type=MESH,
        )

    def flat(buffer, start, count):
        return buffer[pl.ds(start, count)].reshape(count * cols, channels).astype(F32)

    def widen(wide, start, values):
        count = values.shape[0]
        column = lax.rem(lax.broadcasted_iota(jnp.int32, values.shape, 0), cols)
        before = jnp.where(column == 0, 0.0, pltpu.roll(values, 1, 0))
        after = jnp.where(column == cols - 1, 0.0, pltpu.roll(values, count - 1, 0))
        at = pl.ds(start * cols, count)
        wide[at, 0:channels] = before.astype(BF16)
        wide[at, channels : 2 * channels] = values.astype(BF16)
        wide[at, 2 * channels : 3 * channels] = after.astype(BF16)

    def conv(wide, start, count, weight):
        summed = None
        for i in range(3):
            product = jnp.dot(
                wide[pl.ds((start + i) * cols, count * cols), :],
                weight[i].reshape(3 * channels, channels),
                preferred_element_type=F32,
            )
            summed = product if summed is None else summed + product
        return summed

    def conv_back(wide, start, count, weight):
        summed = None
        for i in range(3):
            for j in range(3):
                product = lax.dot_general(
                    wide[pl.ds((start + i) * cols, count * cols), j * channels : (j + 1) * channels],
                    weight[2 - i, 2 - j],
                    (((1,), (1,)), ((), ())),
                    preferred_element_type=F32,
                )
                summed = product if summed is None else summed + product
        return summed

    def moments(summed):
        spread = group_spread(summed, width) / cells
        centre = spread[0:1]
        variance = jnp.maximum(spread[1:2] - centre * centre, 0.0)
        return centre, lax.rsqrt(variance + EPSILON)

    loads[0].wait()
    values = flat(images, REACH, rows)
    sums = column_sums(values, values * values)
    loads[1].wait()
    pl.semaphore_wait(barrier, n - 1 + m - 1)
    share(0, sums)
    for which, buffer in enumerate((images, cot)):

        @pl.when(above)
        def _():
            halo_copy(which, buffer, True).start()

        @pl.when(below)
        def _():
            halo_copy(which, buffer, False).start()

        @pl.when(jnp.logical_not(above))
        def _():
            buffer[pl.ds(0, REACH)] = jnp.zeros((REACH, cols, channels), BF16)

        @pl.when(jnp.logical_not(below))
        def _():
            buffer[pl.ds(rows + REACH, REACH)] = jnp.zeros((REACH, cols, channels), BF16)

    for k in (2, 3, 4, 7, 8, 9, 10):
        loads[k].wait()
    half = tweight.shape[0] // 2
    index = lax.broadcasted_iota(jnp.int32, (half, 1), 0).astype(F32)
    angles = steps_ref[0].astype(F32) * jnp.exp(-math.log(10000.0) * index / half)
    pre_time = (
        jnp.sum(jnp.cos(angles) * tweight[0:half].astype(F32), axis=0, keepdims=True)
        + jnp.sum(jnp.sin(angles) * tweight[half:].astype(F32), axis=0, keepdims=True)
        + tbias_ref[...]
    )
    entry = lax.broadcasted_iota(jnp.int32, table.shape, 0) == ids_ref[0]
    picked = jnp.sum(jnp.where(entry, table[...].astype(F32), 0.0), axis=0, keepdims=True)
    embedding = pre_time * jax.nn.sigmoid(pre_time) + picked
    activated = embedding * jax.nn.sigmoid(embedding)
    acts[mine] = activated
    for k in range(1, m):
        image_copy(acts, act_send, act_recv, k, False).start()
    partial = jnp.dot(
        jnp.broadcast_to(activated, (8, activated.shape[1])),
        aweight[...].astype(F32),
        precision=HIGHEST,
        preferred_element_type=F32,
    )[0:1]
    share(1, jnp.concatenate([partial[:, :channels], partial[:, channels:]], axis=0))

    gain, bias = gain_ref[...], bias_ref[...]
    centre, inverse_first = moments(total(0))

    def first_activation(normed):
        pre = normed * gain + bias
        return pre, jax.nn.sigmoid(pre)

    values = (flat(images, REACH, rows) - centre) * inverse_first
    pre, sigma = first_activation(values)
    widen(wide_first, REACH, pre * sigma)

    def halo_wait(which, buffer):
        @pl.when(below)
        def _():
            halo_copy(which, buffer, True).wait_recv()

        @pl.when(above)
        def _():
            halo_copy(which, buffer, False).wait_recv()

    halo_wait(0, images)
    for start, inside in ((0, above), (rows + REACH, below)):
        rim_values = (flat(images, start, REACH) - centre) * inverse_first
        rim_pre, rim_sigma = first_activation(rim_values)
        widen(wide_first, start, jnp.where(inside, rim_pre * rim_sigma, 0.0))
    loads[5].wait()
    centre_rows = conv(wide_first, 1, rows, first).astype(BF16).astype(F32)
    share(2, column_sums(centre_rows, centre_rows * centre_rows))
    hidden[pl.ds(rim, own)] = centre_rows

    for row in (0, rows + 1):
        hidden[pl.ds(row * cols, cols)] = conv(wide_first, row, 1, first).astype(BF16).astype(F32)
    halo_wait(1, cot)
    widen(wide_cot, 0, flat(cot, 0, rows + 2 * REACH))
    loads[6].wait()
    gact[...] = conv_back(wide_cot, 0, rows + 2, second)
    values = (flat(images, REACH, rows) - centre) * inverse_first
    pre, sigma = first_activation(values)
    nfirst[...] = values
    slope[...] = silu_slope(pre, sigma) * gain

    modulation = total(1)
    factor = 1.0 + (modulation[0:1] + abias_ref[:, :channels])
    shift = modulation[1:2] + abias_ref[:, channels:]
    centre, inverse_second = moments(total(2))
    for start, count, inside in ((1, rows, None), (0, 1, above), (rows + 1, 1, below)):
        at = pl.ds(start * cols, count * cols)
        normed = (hidden[at] - centre) * inverse_second
        pre = normed * factor + shift
        sigma = jax.nn.sigmoid(pre)
        back = gact[at] * silu_slope(pre, sigma)
        if inside is None:
            share(3, column_sums(back * normed, back))
        active = pre * sigma
        if inside is not None:
            active = jnp.where(inside, active, 0.0)
        widen(wide_second, start, active)
        nsecond[at] = normed
        gpre[at] = back

    branch[0] = conv(wide_second, 0, rows, second).astype(BF16).reshape(rows, cols, channels)

    sums = total(3)
    spread = group_spread(sums * factor, width) / cells
    paired_mean, plain_mean = spread[0:1], spread[1:2]
    for start, count, inside in ((1, rows, None), (0, 1, above), (rows + 1, 1, below)):
        at = pl.ds(start * cols, count * cols)
        back = inverse_second * (gpre[at] * factor - plain_mean - nsecond[at] * paired_mean)
        if inside is not None:
            back = jnp.where(inside, back, 0.0)
        widen(wide_hidden, start, back)
    pairs[mine] = sums
    for k in range(1, m):
        image_copy(pairs, pair_send, pair_recv, k, False).start()
    back = conv_back(wide_hidden, 0, rows, first) * slope[...]
    normed = nfirst[...]
    share(4, column_sums(back, back * normed))

    for k in range(1, m):
        image_copy(acts, act_send, act_recv, k, True).wait_recv()
        image_copy(pairs, pair_send, pair_recv, k, True).wait_recv()
    acts_out[...] = acts[...]
    pairs_out[...] = pairs[...]

    spread = group_spread(total(4), width) / cells
    result = inverse_first * (back - spread[0:1] - normed * spread[1:2])
    igrad[0] = result.astype(BF16).reshape(rows, cols, channels)

    for stage in range(5):
        for k in range(1, n):
            tile_copy(stage, k, False).wait_send()
    for k in range(1, m):
        image_copy(acts, act_send, act_recv, k, False).wait_send()
        image_copy(pairs, pair_send, pair_recv, k, False).wait_send()
    for which, buffer in enumerate((images, cot)):

        @pl.when(above)
        def _():
            halo_copy(which, buffer, True).wait_send()

        @pl.when(below)
        def _():
            halo_copy(which, buffer, False).wait_send()

def finish(m, branch_in, igrad_in, acts, pairs, branch_hbm, igrad_hbm, wgrad_hbm, bgrad_ref, wgrad, sem):
    copies = [
        pltpu.make_async_copy(branch_in, branch_hbm, sem.at[0]),
        pltpu.make_async_copy(igrad_in, igrad_hbm, sem.at[1]),
        pltpu.make_async_copy(wgrad, wgrad_hbm, sem.at[2]),
    ]
    copies[0].start()
    copies[1].start()
    channels = pairs.shape[2]
    extra = (-m) % 8

    def stacked(pieces):
        if extra:
            pieces = pieces + [jnp.zeros((extra, pieces[0].shape[1]), F32)]
        return jnp.concatenate(pieces, axis=0)

    left = stacked([acts[k] for k in range(m)])
    for part in range(2):
        right = stacked([pairs[k][part : part + 1] for k in range(m)])
        columns = slice(part * channels, (part + 1) * channels)
        wgrad[:, columns] = lax.dot_general(
            left, right, (((0,), (0,)), ((), ())), precision=HIGHEST, preferred_element_type=F32
        )
        bgrad_ref[:, columns] = jnp.sum(right, axis=0, keepdims=True)
    copies[2].start()
    for copy in copies:
        copy.wait()


def body(
    n, m,
    images, cotangent, timesteps, class_ids, norm_gain, norm_bias, conv_first, conv_second,
    time_weight, time_bias, class_table, adaptive_weight, adaptive_bias,
):
    count, rows, cols, channels = images.shape
    assert count == 1 and rows >= REACH
    emb = time_weight.shape[1]
    vmem = pl.BlockSpec(memory_space=pltpu.VMEM)
    anywhere = pl.BlockSpec(memory_space=pl.ANY)
    padded = rows + 2 * REACH
    own, more, most = rows * cols, (rows + 2) * cols, padded * cols
    dma = pltpu.SemaphoreType.DMA
    branch, igrad, acts, pairs = pl.pallas_call(
        functools.partial(kernel, n, m),
        out_shape=(
            jax.ShapeDtypeStruct(images.shape, BF16),
            jax.ShapeDtypeStruct(images.shape, BF16),
            jax.ShapeDtypeStruct((m, 1, emb), F32),
            jax.ShapeDtypeStruct((m, 2, channels), F32),
        ),
        in_specs=[pl.BlockSpec(memory_space=pltpu.SMEM)] * 2
        + [pl.BlockSpec(memory_space=pltpu.HBM)] * 11,
        out_specs=(vmem,) * 4,
        scratch_shapes=[
            pltpu.VMEM((padded, cols, channels), BF16),
            pltpu.VMEM((padded, cols, channels), BF16),
            pltpu.VMEM(conv_first.shape, BF16),
            pltpu.VMEM(conv_second.shape, BF16),
            pltpu.VMEM(time_weight.shape, BF16),
            pltpu.VMEM(class_table.shape, BF16),
            pltpu.VMEM(adaptive_weight.shape, BF16),
            pltpu.VMEM((1, channels), F32),
            pltpu.VMEM((1, channels), F32),
            pltpu.VMEM((1, emb), F32),
            pltpu.VMEM((1, 2 * channels), F32),
            pltpu.VMEM((most, 3 * channels), BF16),
            pltpu.VMEM((most, 3 * channels), BF16),
            pltpu.VMEM((more, 3 * channels), BF16),
            pltpu.VMEM((more, 3 * channels), BF16),
            pltpu.VMEM((more, channels), F32),
            pltpu.VMEM((more, channels), F32),
            pltpu.VMEM((more, channels), F32),
            pltpu.VMEM((more, channels), F32),
            pltpu.VMEM((own, channels), F32),
            pltpu.VMEM((own, channels), F32),
            pltpu.VMEM((5, n, 2, channels), F32),
            pltpu.VMEM((m, 1, emb), F32),
            pltpu.VMEM((m, 2, channels), F32),
            dma((11,)),
            dma((2, 2)),
            dma((2, 2)),
            dma((5, n)),
            dma((5, n)),
            dma((m,)),
            dma((m,)),
            dma((m,)),
            dma((m,)),
        ],
        compiler_params=pltpu.CompilerParams(
            collective_id=0, has_side_effects=True, vmem_limit_bytes=GRANT
        ),
    )(
        timesteps, class_ids,
        *(
            pltpu.with_memory_space_constraint(operand, pltpu.HBM)
            for operand in (
                norm_gain[None], norm_bias[None], time_bias[None],
                adaptive_bias[None], images, cotangent, conv_first, conv_second, time_weight,
                class_table, adaptive_weight,
            )
        )
    )
    branch, igrad, wgrad, bgrad = pl.pallas_call(
        functools.partial(finish, m),
        out_shape=(
            jax.ShapeDtypeStruct(images.shape, BF16),
            jax.ShapeDtypeStruct(images.shape, BF16),
            jax.ShapeDtypeStruct((emb, 2 * channels), F32),
            jax.ShapeDtypeStruct((1, 2 * channels), F32),
        ),
        in_specs=[anywhere] * 2 + [vmem] * 2,
        out_specs=(anywhere, anywhere, anywhere, vmem),
        scratch_shapes=[pltpu.VMEM((emb, 2 * channels), F32), dma((3,))],
        compiler_params=pltpu.CompilerParams(vmem_limit_bytes=GRANT),
    )(branch, igrad, acts, pairs)
    return branch, igrad, wgrad, bgrad[0]


def solution(mesh):
    return jax.shard_map(
        functools.partial(body, mesh.shape["tile"], mesh.shape["image"]),
        mesh=mesh,
        in_specs=(
            P(("groups", "image"), "tile", None, None),
            P(("groups", "image"), "tile", None, None),
            P(("groups", "image")),
            P(("groups", "image")),
            P(),
            P(),
            P(),
            P(),
            P(None, "tile"),
            P("tile"),
            P(None, "tile"),
            P("tile", None),
            P(),
        ),
        out_specs=(
            P(("groups", "image"), "tile", None, None),
            P(("groups", "image"), "tile", None, None),
            P(("groups", "tile"), None),
            P("groups"),
        ),
        check_vma=False,
    )
```

```python
import functools
import math

import jax
import jax.numpy as jnp
from jax import lax
from jax.experimental import pallas as pl
from jax.experimental.pallas import tpu as pltpu
from jax.sharding import PartitionSpec as P

GN_GROUPS = 32
EPSILON = 1e-05
MESH = pl.DeviceIdType.MESH
F32 = jnp.float32
BF16 = jnp.bfloat16
GRANT = 24 << 20
REACH = 2
HIGHEST = lax.Precision.HIGHEST


def group_spread(values, width):
    count = values.shape[-1]
    lane = lax.broadcasted_iota(jnp.int32, values.shape, values.ndim - 1)
    step = 1
    while step < width:
        up = pltpu.roll(values, step, values.ndim - 1)
        down = pltpu.roll(values, count - step, values.ndim - 1)
        values = values + jnp.where((lane & step) != 0, up, down)
        step *= 2
    return values


def silu_slope(pre, sigma):
    return sigma * (1.0 + pre * (1.0 - sigma))


def column_sums(first, second):
    return jnp.concatenate(
        [jnp.sum(first, axis=0, keepdims=True), jnp.sum(second, axis=0, keepdims=True)], axis=0
    )


def kernel(
    n, m,
    steps_ref, ids_ref, gain_hbm, bias_hbm, tbias_hbm, abias_hbm,
    images_hbm, cot_hbm, first_hbm, second_hbm, tweight_hbm, table_hbm, aweight_hbm,
    branch, igrad, wgrad, bgrad,
    images, cot, first, second, tweight, table, aweight,
    gain_ref, bias_ref, tbias_ref, abias_ref,
    wide_first, wide_cot, wide_second, wide_hidden,
    hidden, gact, nsecond, gpre, nfirst, slope,
    slots, acts, pairs,
    load_sem, halo_send, halo_recv, send_sem, recv_sem,
    act_send, act_recv, pair_send, pair_recv,
):
    me = lax.axis_index("tile")
    mine = lax.axis_index("image")
    rows, cols, channels = images_hbm.shape[1:]
    width = channels // GN_GROUPS
    cells = float(rows * cols * n * width)
    own = rows * cols
    rim = cols
    above, below = me > 0, me < n - 1

    loads = [
        pltpu.make_async_copy(source, target, load_sem.at[k])
        for k, (source, target) in enumerate(
            [
                (images_hbm.at[0], images.at[pl.ds(REACH, rows)]),
                (cot_hbm.at[0], cot.at[pl.ds(REACH, rows)]),
                (tweight_hbm, tweight),
                (table_hbm, table),
                (aweight_hbm, aweight),
                (first_hbm, first),
                (second_hbm, second),
                (gain_hbm, gain_ref),
                (bias_hbm, bias_ref),
                (tbias_hbm, tbias_ref),
                (abias_hbm, abias_ref),
            ]
        )
    ]
    for load in loads:
        load.start()

    barrier = pltpu.get_barrier_semaphore()
    for k in range(1, n):
        pl.semaphore_signal(
            barrier, inc=1, device_id={"tile": lax.rem(me + k, n)}, device_id_type=MESH
        )
    for k in range(1, m):
        pl.semaphore_signal(
            barrier, inc=1, device_id={"image": lax.rem(mine + k, m)}, device_id_type=MESH
        )

    def tile_copy(stage, k, arriving):
        peer = lax.rem(me + k, n)
        slot = lax.rem(me + n - k, n) if arriving else me
        return pltpu.make_async_remote_copy(
            src_ref=slots.at[stage, slot],
            dst_ref=slots.at[stage, slot],
            send_sem=send_sem.at[stage, k],
            recv_sem=recv_sem.at[stage, k],
            device_id={"tile": peer},
            device_id_type=MESH,
        )

    def share(stage, value):
        slots[stage, me] = value
        for k in range(1, n):
            tile_copy(stage, k, False).start()

    def total(stage):
        for k in range(1, n):
            tile_copy(stage, k, True).wait_recv()
        summed = slots[stage, 0]
        for k in range(1, n):
            summed = summed + slots[stage, k]
        return summed

    def image_copy(buffer, sends, receives, k, arriving):
        peer = lax.rem(mine + k, m)
        slot = lax.rem(mine + m - k, m) if arriving else mine
        return pltpu.make_async_remote_copy(
            src_ref=buffer.at[slot],
            dst_ref=buffer.at[slot],
            send_sem=sends.at[k],
            recv_sem=receives.at[k],
            device_id={"image": peer},
            device_id_type=MESH,
        )

    def halo_copy(which, buffer, up):
        source = pl.ds(REACH, REACH) if up else pl.ds(rows, REACH)
        target = pl.ds(rows + REACH, REACH) if up else pl.ds(0, REACH)
        return pltpu.make_async_remote_copy(
            src_ref=buffer.at[source],
            dst_ref=buffer.at[target],
            send_sem=halo_send.at[which, int(up)],
            recv_sem=halo_recv.at[which, int(up)],
            device_id={"tile": me - 1 if up else me + 1},
            device_id_type=MESH,
        )

    def flat(buffer, start, count):
        return buffer[pl.ds(start, count)].reshape(count * cols, channels).astype(F32)

    def widen(wide, start, values):
        count = values.shape[0]
        column = lax.rem(lax.broadcasted_iota(jnp.int32, values.shape, 0), cols)
        before = jnp.where(column == 0, 0.0, pltpu.roll(values, 1, 0))
        after = jnp.where(column == cols - 1, 0.0, pltpu.roll(values, count - 1, 0))
        at = pl.ds(start * cols, count)
        wide[at, 0:channels] = before.astype(BF16)
        wide[at, channels : 2 * channels] = values.astype(BF16)
        wide[at, 2 * channels : 3 * channels] = after.astype(BF16)

    def conv(wide, start, count, weight):
        summed = None
        for i in range(3):
            product = jnp.dot(
                wide[pl.ds((start + i) * cols, count * cols), :],
                weight[i].reshape(3 * channels, channels),
                preferred_element_type=F32,
            )
            summed = product if summed is None else summed + product
        return summed

    def conv_back(wide, start, count, weight):
        summed = None
        for i in range(3):
            for j in range(3):
                product = lax.dot_general(
                    wide[pl.ds((start + i) * cols, count * cols), j * channels : (j + 1) * channels],
                    weight[2 - i, 2 - j],
                    (((1,), (1,)), ((), ())),
                    preferred_element_type=F32,
                )
                summed = product if summed is None else summed + product
        return summed

    def moments(summed):
        spread = group_spread(summed, width) / cells
        centre = spread[0:1]
        variance = jnp.maximum(spread[1:2] - centre * centre, 0.0)
        return centre, lax.rsqrt(variance + EPSILON)

    loads[0].wait()
    values = flat(images, REACH, rows)
    sums = column_sums(values, values * values)
    pl.semaphore_wait(barrier, n - 1 + m - 1)
    share(0, sums)
    def halo_start(which, buffer):

        @pl.when(above)
        def _():
            halo_copy(which, buffer, True).start()

        @pl.when(below)
        def _():
            halo_copy(which, buffer, False).start()

        @pl.when(jnp.logical_not(above))
        def _():
            buffer[pl.ds(0, REACH)] = jnp.zeros((REACH, cols, channels), BF16)

        @pl.when(jnp.logical_not(below))
        def _():
            buffer[pl.ds(rows + REACH, REACH)] = jnp.zeros((REACH, cols, channels), BF16)

    halo_start(0, images)

    for k in (2, 3, 4, 7, 8, 9, 10):
        loads[k].wait()
    half = tweight.shape[0] // 2
    index = lax.broadcasted_iota(jnp.int32, (half, 1), 0).astype(F32)
    angles = steps_ref[0].astype(F32) * jnp.exp(-math.log(10000.0) * index / half)
    pre_time = (
        jnp.sum(jnp.cos(angles) * tweight[0:half].astype(F32), axis=0, keepdims=True)
        + jnp.sum(jnp.sin(angles) * tweight[half:].astype(F32), axis=0, keepdims=True)
        + tbias_ref[...]
    )
    entry = lax.broadcasted_iota(jnp.int32, table.shape, 0) == ids_ref[0]
    picked = jnp.sum(jnp.where(entry, table[...].astype(F32), 0.0), axis=0, keepdims=True)
    embedding = pre_time * jax.nn.sigmoid(pre_time) + picked
    activated = embedding * jax.nn.sigmoid(embedding)
    acts[mine] = activated
    for k in range(1, m):
        image_copy(acts, act_send, act_recv, k, False).start()
    partial = jnp.dot(
        jnp.broadcast_to(activated, (8, activated.shape[1])),
        aweight[...].astype(F32),
        precision=HIGHEST,
        preferred_element_type=F32,
    )[0:1]
    share(1, jnp.concatenate([partial[:, :channels], partial[:, channels:]], axis=0))

    loads[1].wait()
    halo_start(1, cot)

    gain, bias = gain_ref[...], bias_ref[...]
    centre, inverse_first = moments(total(0))

    def first_activation(normed):
        pre = normed * gain + bias
        return pre, jax.nn.sigmoid(pre)

    values = (flat(images, REACH, rows) - centre) * inverse_first
    pre, sigma = first_activation(values)
    widen(wide_first, REACH, pre * sigma)

    def halo_wait(which, buffer):
        @pl.when(below)
        def _():
            halo_copy(which, buffer, True).wait_recv()

        @pl.when(above)
        def _():
            halo_copy(which, buffer, False).wait_recv()

    halo_wait(0, images)
    for start, inside in ((0, above), (rows + REACH, below)):
        rim_values = (flat(images, start, REACH) - centre) * inverse_first
        rim_pre, rim_sigma = first_activation(rim_values)
        widen(wide_first, start, jnp.where(inside, rim_pre * rim_sigma, 0.0))
    loads[5].wait()
    centre_rows = conv(wide_first, 1, rows, first).astype(BF16).astype(F32)
    share(2, column_sums(centre_rows, centre_rows * centre_rows))
    hidden[pl.ds(rim, own)] = centre_rows

    for row in (0, rows + 1):
        hidden[pl.ds(row * cols, cols)] = conv(wide_first, row, 1, first).astype(BF16).astype(F32)
    halo_wait(1, cot)
    widen(wide_cot, 0, flat(cot, 0, rows + 2 * REACH))
    loads[6].wait()
    gact[...] = conv_back(wide_cot, 0, rows + 2, second)
    values = (flat(images, REACH, rows) - centre) * inverse_first
    pre, sigma = first_activation(values)
    nfirst[...] = values
    slope[...] = silu_slope(pre, sigma) * gain

    modulation = total(1)
    factor = 1.0 + (modulation[0:1] + abias_ref[:, :channels])
    shift = modulation[1:2] + abias_ref[:, channels:]
    centre, inverse_second = moments(total(2))
    for start, count, inside in ((1, rows, None), (0, 1, above), (rows + 1, 1, below)):
        at = pl.ds(start * cols, count * cols)
        normed = (hidden[at] - centre) * inverse_second
        pre = normed * factor + shift
        sigma = jax.nn.sigmoid(pre)
        back = gact[at] * silu_slope(pre, sigma)
        if inside is None:
            share(3, column_sums(back * normed, back))
        active = pre * sigma
        if inside is not None:
            active = jnp.where(inside, active, 0.0)
        widen(wide_second, start, active)
        nsecond[at] = normed
        gpre[at] = back

    branch[0] = conv(wide_second, 0, rows, second).astype(BF16).reshape(rows, cols, channels)

    sums = total(3)
    spread = group_spread(sums * factor, width) / cells
    paired_mean, plain_mean = spread[0:1], spread[1:2]
    for start, count, inside in ((1, rows, None), (0, 1, above), (rows + 1, 1, below)):
        at = pl.ds(start * cols, count * cols)
        back = inverse_second * (gpre[at] * factor - plain_mean - nsecond[at] * paired_mean)
        if inside is not None:
            back = jnp.where(inside, back, 0.0)
        widen(wide_hidden, start, back)
    pairs[mine] = sums
    for k in range(1, m):
        image_copy(pairs, pair_send, pair_recv, k, False).start()
    back = conv_back(wide_hidden, 0, rows, first) * slope[...]
    normed = nfirst[...]
    share(4, column_sums(back, back * normed))

    for k in range(1, m):
        image_copy(acts, act_send, act_recv, k, True).wait_recv()
        image_copy(pairs, pair_send, pair_recv, k, True).wait_recv()
    extra = (-m) % 8

    def stacked(pieces):
        if extra:
            pieces = pieces + [jnp.zeros((extra, pieces[0].shape[1]), F32)]
        return jnp.concatenate(pieces, axis=0)

    left = stacked([acts[k] for k in range(m)])
    for part in range(2):
        right = stacked([pairs[k][part : part + 1] for k in range(m)])
        columns = slice(part * channels, (part + 1) * channels)
        wgrad[:, columns] = lax.dot_general(
            left, right, (((0,), (0,)), ((), ())), precision=HIGHEST, preferred_element_type=F32
        )
        bgrad[:, columns] = jnp.sum(right, axis=0, keepdims=True)

    spread = group_spread(total(4), width) / cells
    result = inverse_first * (back - spread[0:1] - normed * spread[1:2])
    igrad[0] = result.astype(BF16).reshape(rows, cols, channels)

    for stage in range(5):
        for k in range(1, n):
            tile_copy(stage, k, False).wait_send()
    for k in range(1, m):
        image_copy(acts, act_send, act_recv, k, False).wait_send()
        image_copy(pairs, pair_send, pair_recv, k, False).wait_send()
    for which, buffer in enumerate((images, cot)):

        @pl.when(above)
        def _():
            halo_copy(which, buffer, True).wait_send()

        @pl.when(below)
        def _():
            halo_copy(which, buffer, False).wait_send()

def finish(*refs):
    count = (len(refs) - 1) // 2
    sem = refs[-1]
    copies = [
        pltpu.make_async_copy(refs[k], refs[count + k], sem.at[k]) for k in range(count)
    ]
    for copy in copies:
        copy.start()
    for copy in copies:
        copy.wait()


def body(
    n, m,
    images, cotangent, timesteps, class_ids, norm_gain, norm_bias, conv_first, conv_second,
    time_weight, time_bias, class_table, adaptive_weight, adaptive_bias,
):
    count, rows, cols, channels = images.shape
    assert count == 1 and rows >= REACH
    emb = time_weight.shape[1]
    vmem = pl.BlockSpec(memory_space=pltpu.VMEM)
    anywhere = pl.BlockSpec(memory_space=pl.ANY)
    padded = rows + 2 * REACH
    own, more, most = rows * cols, (rows + 2) * cols, padded * cols
    dma = pltpu.SemaphoreType.DMA
    results = pl.pallas_call(
        functools.partial(kernel, n, m),
        out_shape=(
            jax.ShapeDtypeStruct(images.shape, BF16),
            jax.ShapeDtypeStruct(images.shape, BF16),
            jax.ShapeDtypeStruct((emb, 2 * channels), F32),
            jax.ShapeDtypeStruct((1, 2 * channels), F32),
        ),
        in_specs=[pl.BlockSpec(memory_space=pltpu.SMEM)] * 2
        + [pl.BlockSpec(memory_space=pltpu.HBM)] * 11,
        out_specs=(vmem,) * 4,
        scratch_shapes=[
            pltpu.VMEM((padded, cols, channels), BF16),
            pltpu.VMEM((padded, cols, channels), BF16),
            pltpu.VMEM(conv_first.shape, BF16),
            pltpu.VMEM(conv_second.shape, BF16),
            pltpu.VMEM(time_weight.shape, BF16),
            pltpu.VMEM(class_table.shape, BF16),
            pltpu.VMEM(adaptive_weight.shape, BF16),
            pltpu.VMEM((1, channels), F32),
            pltpu.VMEM((1, channels), F32),
            pltpu.VMEM((1, emb), F32),
            pltpu.VMEM((1, 2 * channels), F32),
            pltpu.VMEM((most, 3 * channels), BF16),
            pltpu.VMEM((most, 3 * channels), BF16),
            pltpu.VMEM((more, 3 * channels), BF16),
            pltpu.VMEM((more, 3 * channels), BF16),
            pltpu.VMEM((more, channels), F32),
            pltpu.VMEM((more, channels), F32),
            pltpu.VMEM((more, channels), F32),
            pltpu.VMEM((more, channels), F32),
            pltpu.VMEM((own, channels), F32),
            pltpu.VMEM((own, channels), F32),
            pltpu.VMEM((5, n, 2, channels), F32),
            pltpu.VMEM((m, 1, emb), F32),
            pltpu.VMEM((m, 2, channels), F32),
            dma((11,)),
            dma((2, 2)),
            dma((2, 2)),
            dma((5, n)),
            dma((5, n)),
            dma((m,)),
            dma((m,)),
            dma((m,)),
            dma((m,)),
        ],
        compiler_params=pltpu.CompilerParams(
            collective_id=0, has_side_effects=True, vmem_limit_bytes=GRANT
        ),
    )(
        timesteps, class_ids,
        *(
            pltpu.with_memory_space_constraint(operand, pltpu.HBM)
            for operand in (
                norm_gain[None], norm_bias[None], time_bias[None],
                adaptive_bias[None], images, cotangent, conv_first, conv_second, time_weight,
                class_table, adaptive_weight,
            )
        )
    )
    branch, igrad, wgrad, bgrad = pl.pallas_call(
        finish,
        out_shape=tuple(jax.ShapeDtypeStruct(r.shape, r.dtype) for r in results),
        in_specs=[anywhere] * 4,
        out_specs=(anywhere,) * 4,
        scratch_shapes=[dma((4,))],
        compiler_params=pltpu.CompilerParams(vmem_limit_bytes=GRANT),
    )(*results)
    return branch, igrad, wgrad, bgrad[0]


def solution(mesh):
    return jax.shard_map(
        functools.partial(body, mesh.shape["tile"], mesh.shape["image"]),
        mesh=mesh,
        in_specs=(
            P(("groups", "image"), "tile", None, None),
            P(("groups", "image"), "tile", None, None),
            P(("groups", "image")),
            P(("groups", "image")),
            P(),
            P(),
            P(),
            P(),
            P(None, "tile"),
            P("tile"),
            P(None, "tile"),
            P("tile", None),
            P(),
        ),
        out_specs=(
            P(("groups", "image"), "tile", None, None),
            P(("groups", "image"), "tile", None, None),
            P(("groups", "tile"), None),
            P("groups"),
        ),
        check_vma=False,
    )
```
